256 devices in a mesh: line: 4 (over y), patch: 64 (over x, z, core).
Axes of the slice: x: 4, y: 4, z: 8, core: 2. Of those that a mesh axis runs over, the one named last changes fastest.
Arguments:
- newton_residual: float32 [8, 48, 64, 128], P('line', None, 'patch'), may hold values from -24 to 24
- diag_block: bfloat16 [8, 48, 48, 64, 128], P('line', None, None, 'patch'), may hold values from -0.6 to 5
- lower: bfloat16 [8, 48, 48, 64, 128], P('line', None, None, 'patch'), may hold values from -1.296875 to 1.296875
- upper: bfloat16 [8, 48, 48, 64, 128], P('line', None, None, 'patch'), may hold values from -1.296875 to 1.296875
- west: bfloat16 [8, 48, 48, 64, 128], P('line', None, None, 'patch'), may hold values from -0.5390625 to 0.5390625
- east: bfloat16 [8, 48, 48, 64, 128], P('line', None, None, 'patch'), may hold values from -0.5390625 to 0.5390625
- pivot_inverse: bfloat16 [8, 48, 48, 64, 128], P('line', None, None, 'patch'), may hold values from -0.05 to 0.34
Outputs:
- newton_step: float32 [8, 48, 64, 128], P('line', None, 'patch')
The draws below stay inside these ranges and needn't reach their ends.
All inputs are finite; a program needn't handle non-finite values.
Results may differ from the reference program's by a relative error of at most 0.0003.
Values sent between devices are 32-bit elements; how exact they have to be, the bound alone decides.
A program may use at most 64 MiB of HBM per device.

```python
import math
import jax
import jax.numpy as jnp
from jax import lax

BLOCK = 48
ACROSS = 128
ITERS = 4
LEN = 8
ROWS = 64


def draw_diag_block(key, part):
    first_key, second_key = jax.random.split(jax.random.fold_in(key, 11))
    diagonal = jax.random.uniform(first_key, (LEN, BLOCK, ROWS, ACROSS), jnp.float32, 3.0, 5.0)
    spread = jnp.clip(jax.random.normal(second_key, (LEN, BLOCK, BLOCK, ROWS, ACROSS), jnp.float32), -4.0, 4.0)
    spread = spread / math.sqrt(BLOCK)
    identity = jnp.eye(BLOCK, dtype=jnp.float32)[None, :, :, None, None]
    whole = spread * (1.0 - identity) + identity * diagonal[:, :, None, :, :]
    return whole.astype(jnp.bfloat16)


def draw_pivot_inverse(key, part):
    first_key, second_key = jax.random.split(jax.random.fold_in(key, 23))
    diagonal = jnp.exp(jax.random.uniform(first_key, (LEN, BLOCK, ROWS, ACROSS), jnp.float32, math.log(0.2), math.log(0.33)))
    spread = jnp.clip(jax.random.normal(second_key, (LEN, BLOCK, BLOCK, ROWS, ACROSS), jnp.float32), -4.0, 4.0)
    spread = spread * (0.08 / math.sqrt(BLOCK))
    identity = jnp.eye(BLOCK, dtype=jnp.float32)[None, :, :, None, None]
    whole = spread * (1.0 - identity) + identity * diagonal[:, :, None, :, :]
    return whole.astype(jnp.bfloat16)


def block_levels(rng, dims, pieces, low, high):
    level = 1.0
    for position, parts in pieces:
        steps = jax.random.uniform(jax.random.fold_in(jax.random.fold_in(rng, 6), position), (parts,), jnp.float32, low / len(pieces), high / len(pieces))
        level = level * jnp.repeat(jnp.exp(steps), dims[position] // parts).reshape((-1,) + (1,) * (len(dims) - 1 - position))
    return level


def bell_draw(rng, extent, deviation, most, shards=(), held_as=jnp.bfloat16):
    array = deviation * jax.random.normal(rng, extent, jnp.float32)
    if shards:
        array = array * block_levels(rng, extent, shards, -0.22, 0.18)
    return jnp.clip(array, -most, most).astype(held_as)


def setup_inputs(seed: int = 0) -> dict:
    splits = jax.random.split(jax.random.key(seed), 8)
    return {
        "newton_residual": bell_draw(splits[0], (LEN, BLOCK, ROWS, ACROSS), 4.0, 24.0, ((0, 4), (2, 64)), jnp.float32),
        "diag_block": draw_diag_block(jax.random.fold_in(splits[7], 71), 0),
        "lower": bell_draw(splits[2], (LEN, BLOCK, BLOCK, ROWS, ACROSS), 0.22, 1.296875, ((0, 4), (3, 64))),
        "upper": bell_draw(splits[3], (LEN, BLOCK, BLOCK, ROWS, ACROSS), 0.22, 1.296875, ((0, 4), (3, 64))),
        "west": bell_draw(splits[4], (LEN, BLOCK, BLOCK, ROWS, ACROSS), 0.09, 0.5390625, ((0, 4), (3, 64))),
        "east": bell_draw(splits[5], (LEN, BLOCK, BLOCK, ROWS, ACROSS), 0.09, 0.5390625, ((0, 4), (3, 64))),
        "pivot_inverse": draw_pivot_inverse(jax.random.fold_in(splits[7], 71), 0),
    }


def block_apply(block_mat, vector):
    return lax.map(lambda couple: lax.optimization_barrier(jnp.sum(couple[0].astype(jnp.float32) * couple[1][None], axis=1)), (block_mat, vector))

def single_apply(block_mat, vector):
    return lax.optimization_barrier(jnp.sum(block_mat.astype(jnp.float32) * vector[None], axis=1))

def operator_apply(field, diag_block, lower, upper, west, east):
    zero_layer = jnp.zeros_like(field[:1])
    below = jnp.concatenate([zero_layer, field[:-1]], axis=0)
    above = jnp.concatenate([field[1:], zero_layer], axis=0)
    zero_row = jnp.zeros_like(field[:, :, :1])
    before = jnp.concatenate([zero_row, field[:, :, :-1]], axis=2)
    after = jnp.concatenate([field[:, :, 1:], zero_row], axis=2)
    total = block_apply(diag_block, field) + block_apply(lower, below) + block_apply(upper, above)
    return total + block_apply(west, before) + block_apply(east, after)

def line_solve(vector, lower, upper, pivot):
    count = vector.shape[0]
    previous = jnp.zeros_like(vector[0])
    forward = []
    for k in range(count):
        previous = single_apply(pivot[k], vector[k] - single_apply(lower[k], previous))
        forward.append(previous)
    following = jnp.zeros_like(vector[0])
    result = [None] * count
    for k in reversed(range(count)):
        following = forward[k] - single_apply(pivot[k], single_apply(upper[k], following))
        result[k] = following
    return jnp.stack(result)

def least_squares(hess, beta):
    width = hess.shape[1]
    hess_rows = [hess[i] for i in range(width + 1)]
    target = [beta] + [jnp.zeros((), jnp.float32) for i in range(width)]
    for j in range(width):
        first = hess_rows[j][j]
        second = hess_rows[j + 1][j]
        radius = jnp.sqrt(first * first + second * second)
        cosine = first / radius
        sine_part = second / radius
        upper_row = cosine * hess_rows[j] + sine_part * hess_rows[j + 1]
        lower_row = cosine * hess_rows[j + 1] - sine_part * hess_rows[j]
        hess_rows[j] = upper_row
        hess_rows[j + 1] = lower_row
        top_value = cosine * target[j] + sine_part * target[j + 1]
        low_value = cosine * target[j + 1] - sine_part * target[j]
        target[j] = top_value
        target[j + 1] = low_value
    solution = [None] * width
    for i in reversed(range(width)):
        accum_value = target[i]
        for k in range(i + 1, width):
            accum_value = accum_value - hess_rows[i][k] * solution[k]
        solution[i] = accum_value / hess_rows[i][i]
    return solution

def reference(newton_residual, diag_block, lower, upper, west, east, pivot_inverse):
    beta = jnp.sqrt(jnp.sum(newton_residual * newton_residual))
    basis = [newton_residual / beta]
    directions = []
    columns = []
    for j in range(ITERS):
        direction = line_solve(basis[j], lower, upper, pivot_inverse)
        directions.append(direction)
        image = operator_apply(direction, diag_block, lower, upper, west, east)
        projections = jnp.stack([jnp.sum(member * image) for member in basis])
        for i in range(j + 1):
            image = image - projections[i] * basis[i]
        new_norm = jnp.sqrt(jnp.sum(image * image))
        basis.append(image / new_norm)
        columns.append(jnp.concatenate([projections, new_norm[None], jnp.zeros((ITERS - 1 - j,), jnp.float32)]))
    hess = jnp.stack(columns, axis=1)
    coeffs = least_squares(hess, beta)
    newton_step = coeffs[0] * directions[0]
    for j in range(1, ITERS):
        newton_step = newton_step + coeffs[j] * directions[j]
    return newton_step
```

```python
import functools

import jax
import jax.numpy as jnp
from jax import lax
from jax.experimental import pallas as pl
from jax.experimental.pallas import tpu as pltpu
from jax.sharding import PartitionSpec as P

MESH = pl.DeviceIdType.MESH
F32 = jnp.float32
B = 48
N = 4
SCALE = 2.0**-15
PIV, LOW, UP, DIAG, WEST, EAST = range(6)
GROUP = 16


def kernel(
    lines, rows,
    r_hbm, piv_hbm, low_hbm, up_hbm, diag_hbm, west_hbm, east_hbm,
    out_ref,
    packed, mats, xin, u, d, z, g, gin, zin, zlow, hw, he, bacc, tmp,
    part1, recv1, part2, recv2, res, gam, coef, eta,
    load_sem, carry_send, carry_recv, up_send, up_recv, low_send, low_recv,
    west_send, west_recv, east_send, east_recv, red1_send, red1_recv, red2_send, red2_recv,
):
    y = lax.axis_index("line")
    p = lax.axis_index("patch")
    hbm = (piv_hbm, low_hbm, up_hbm, diag_hbm, west_hbm, east_hbm)

    def load(a, k):
        return pltpu.make_async_copy(hbm[a].at[k], packed.at[a, k], load_sem.at[a, k])

    load_r = pltpu.make_async_copy(r_hbm, tmp, load_sem.at[6, 0])
    load_r.start()
    for a in range(6):
        for k in range(2):
            load(a, k).start()

    x, b = p // GROUP, p % GROUP
    a_me = y * 4 + x

    def peer1(o):
        i = lax.rem(a_me + o, GROUP)
        return (i // 4, (i % 4) * GROUP + b)

    def peer2(o):
        return (y, x * GROUP + lax.rem(b + o, GROUP))

    has_down, has_up = y > 0, y < lines - 1
    has_west, has_east = p > 0, p < rows - 1

    barrier = pltpu.get_barrier_semaphore()
    for o in range(1, GROUP):
        pl.semaphore_signal(barrier, inc=1, device_id=peer1(o), device_id_type=MESH)
        pl.semaphore_signal(barrier, inc=1, device_id=peer2(o), device_id_type=MESH)

    @pl.when(has_west)
    def _():
        pl.semaphore_signal(barrier, inc=1, device_id=(y, p - 1), device_id_type=MESH)

    @pl.when(has_east)
    def _():
        pl.semaphore_signal(barrier, inc=1, device_id=(y, p + 1), device_id_type=MESH)

    u[...] = jnp.zeros_like(u)
    d[...] = jnp.zeros_like(d)
    xin[1:] = jnp.zeros_like(xin[1:])
    part1[...] = jnp.zeros_like(part1)
    coef[...] = jnp.zeros_like(coef)
    eta[...] = jnp.ones_like(eta)
    gam[...] = jnp.ones_like(gam)

    @pl.when(jnp.logical_not(has_west))
    def _():
        hw[...] = jnp.zeros_like(hw)

    @pl.when(jnp.logical_not(has_east))
    def _():
        he[...] = jnp.zeros_like(he)

    @pl.when(jnp.logical_not(has_down))
    def _():
        zlow[...] = jnp.zeros_like(zlow)

    load_r.wait()
    xin[0] = tmp[...] * SCALE

    def widen(a, k):
        def body(t, carry):
            for s in range(4):
                i = t * 4 + s
                mats[a, k, pl.ds(i, B, stride=B), :] = packed[a, k, i].astype(F32)
            return carry
        lax.fori_loop(0, B // 4, body, 0)

    def widen_all(first, last):
        for a in range(first, last):
            for k in range(2):
                load(a, k).wait()
        def body(t, carry):
            widen(t // 2, t % 2)
            return carry
        lax.fori_loop(2 * first, 2 * last, body, 0)

    def apply(pairs, start=None):
        step = 8
        def body(t, accs):
            accs = list(accs)
            for s in range(step):
                j = t * step + s
                for a, k, v in pairs:
                    row = v[pl.ds(j, 8, stride=0), :]
                    block = mats[a, k, pl.ds(pl.multiple_of(j * B, 8), B), :].reshape(6, 8, 128)
                    accs[s % 2] = accs[s % 2] + block * row[None]
            return tuple(accs)
        zero = jnp.zeros((6, 8, 128), F32)
        one = zero if start is None else start.reshape(6, 8, 128)
        one, two = lax.fori_loop(0, B // step, body, (one, zero))
        return (one + two).reshape(B, 128)

    def send(src, dst, ssem, rsem, to):
        return pltpu.make_async_remote_copy(
            src_ref=src, dst_ref=dst, send_sem=ssem, recv_sem=rsem, device_id=to, device_id_type=MESH
        )

    def send_carry(n):
        return send(g.at[n, 1], gin.at[n], carry_send.at[n], carry_recv.at[n], (y + 1, p))

    def send_up(n):
        return send(z.at[n, 0], zin.at[n], up_send.at[n], up_recv.at[n], (y - 1, p))

    def send_low(n):
        return send(z.at[n, 1], zlow.at[n], low_send.at[n], low_recv.at[n], (y + 1, p))

    def send_west(n, k):
        return send(z.at[n, k], he.at[n, k], west_send.at[n, k], west_recv.at[n, k], (y, p - 1))

    def send_east(n, k):
        return send(z.at[n, k], hw.at[n, k], east_send.at[n, k], east_recv.at[n, k], (y, p + 1))

    def down_rest(n):
        tmp[0] = xin[n, 1] - apply([(LOW, 1, g.at[n, 0])])
        g[n, 1] = apply([(PIV, 1, tmp.at[0])])

    def red_start(m):
        q0, q1 = xin[m + 1, 0].reshape(6, 8, 128), xin[m + 1, 1].reshape(6, 8, 128)

        def row(i, a0, a1, b0, b1):
            s = jnp.sum(a0 * b0 + a1 * b1, axis=0)
            part1[m, pl.ds(i, 1), :] = jnp.sum(s, axis=0, keepdims=True)

        for i in range(N):
            row(i, u[i, 0].reshape(6, 8, 128), u[i, 1].reshape(6, 8, 128), q0, q1)
        v0, v1 = u[m, 0].reshape(6, 8, 128), u[m, 1].reshape(6, 8, 128)
        row(4, v0, v1, v0, v1)
        row(5, q0, q1, q0, q1)
        for o in range(1, GROUP):
            send(part1.at[m], recv1.at[m, o - 1], red1_send.at[m], red1_recv.at[m], peer1(o)).start()

    def red_middle(m):
        pltpu.make_async_copy(recv1.at[m], recv1.at[m], red1_recv.at[m]).wait()
        part2[m] = part1[m] + jnp.sum(recv1[m], axis=0)
        for o in range(1, GROUP):
            send(part2.at[m], recv2.at[m, o - 1], red2_send.at[m], red2_recv.at[m], peer2(o)).start()

    def red_end(m):
        pltpu.make_async_copy(recv2.at[m], recv2.at[m], red2_recv.at[m]).wait()
        total = part2[m] + jnp.sum(recv2[m], axis=0)
        res[m] = jnp.broadcast_to(jnp.sum(total, axis=1, keepdims=True), (8, 128))
        gam[m] = res[m, pl.ds(4, 8, stride=0), :]
        for i in range(N):
            value = res[m, pl.ds(i, 8, stride=0), :] / gam[i]
            coef[i] = jnp.where(m >= i, value, 0.0)
        eta[...] = 1.0 / jnp.sqrt(res[m, pl.ds(5, 8, stride=0), :])

    def combined(value, olds):
        total = value.reshape(6, 8, 128)
        for i in range(N):
            total = total - coef[i][None] * olds(i).reshape(6, 8, 128)
        return (total * eta[...][None]).reshape(B, 128)

    widen_all(0, 2)

    @pl.when(has_down)
    def _():
        widen_all(2, 6)

    first = True

    def stage(n, carry):
        @pl.when(jnp.logical_not(has_down))
        def _():
            g[n, 0] = apply([(PIV, 0, xin.at[n, 0])])
            down_rest(n)

        @pl.when(n == 0)
        def _():
            pl.semaphore_wait(barrier, 2 * (GROUP - 1) + has_west.astype(jnp.int32) + has_east.astype(jnp.int32))

        @pl.when(jnp.logical_not(has_down))
        def _():
            send_carry(n).start()

            @pl.when(n == 0)
            def _():
                widen_all(2, 6)

        @pl.when(n > 0)
        def _():
            red_start(n - 1)

        @pl.when(has_down)
        def _():
            send_carry(n).wait_recv()
            tmp[1] = xin[n, 0] - apply([(LOW, 0, gin.at[n])])
            g[n, 0] = apply([(PIV, 0, tmp.at[1])])
            down_rest(n)

            @pl.when(has_up)
            def _():
                send_carry(n).start()

        @pl.when(jnp.logical_and(n > 0, has_up))
        def _():
            red_middle(n - 1)

        @pl.when(has_up)
        def _():
            send_up(n).wait_recv()
            bacc[1] = apply([(UP, 1, zin.at[n])])
            z[n, 1] = g[n, 1] - apply([(PIV, 1, bacc.at[1])])
            send_low(n).start()

        @pl.when(jnp.logical_not(has_up))
        def _():
            bacc[1] = jnp.zeros((B, 128), F32)
            z[n, 1] = g[n, 1]

        @pl.when(has_west)
        def _():
            send_west(n, 1).start()

        @pl.when(has_east)
        def _():
            send_east(n, 1).start()

        bacc[0] = apply([(UP, 0, z.at[n, 1])])
        z[n, 0] = g[n, 0] - apply([(PIV, 0, bacc.at[0])])

        @pl.when(has_down)
        def _():
            send_up(n).start()

        @pl.when(has_west)
        def _():
            send_west(n, 0).start()

        @pl.when(has_east)
        def _():
            send_east(n, 0).start()

        @pl.when(jnp.logical_and(n > 0, jnp.logical_not(has_up)))
        def _():
            red_middle(n - 1)

        bacc[1] = apply([(DIAG, 1, z.at[n, 1]), (LOW, 1, z.at[n, 0])], bacc[1])
        bacc[0] = apply([(DIAG, 0, z.at[n, 0])], bacc[0])

        @pl.when(n > 0)
        def _():
            red_end(n - 1)

        for k in range(2):
            u[n, k] = combined(xin[n, k], lambda i: u[i, k])
            d[n, k] = combined(z[n, k], lambda i: d[i, k])

        def halo(k):
            @pl.when(has_west)
            def _():
                send_east(n, k).wait_recv()

            @pl.when(has_east)
            def _():
                send_west(n, k).wait_recv()

        halo(1)
        value = apply([(WEST, 1, hw.at[n, 1]), (EAST, 1, he.at[n, 1])], bacc[1])
        xin[n + 1, 1] = combined(value, lambda i: xin[i + 1, 1])

        @pl.when(has_down)
        def _():
            send_low(n).wait_recv()
            bacc[0] = apply([(LOW, 0, zlow.at[n])], bacc[0])

        halo(0)
        value = apply([(WEST, 0, hw.at[n, 0]), (EAST, 0, he.at[n, 0])], bacc[0])
        xin[n + 1, 0] = combined(value, lambda i: xin[i + 1, 0])
        return carry

    lax.fori_loop(0, N, stage, 0)
    red_start(N - 1)
    red_middle(N - 1)
    red_end(N - 1)

    size = [jnp.sqrt(gam[i]) for i in range(N)]
    zero = jnp.zeros((8, 128), F32)

    def entry(m, i):
        return res[m, pl.ds(i, 8, stride=0), :]

    hess = [[zero] * N for _ in range(N + 1)]
    for m in range(N):
        for i in range(m + 1):
            hess[i][m] = entry(m, i) / (size[i] * size[m])
        if m < N - 1:
            hess[m + 1][m] = size[m + 1] * jnp.sqrt(entry(m, 5)) / size[m]
        else:
            rest = entry(m, 5)
            for i in range(N):
                rest = rest - entry(m, i) * entry(m, i) / gam[i]
            hess[N][m] = jnp.sqrt(jnp.maximum(rest, 0.0)) / size[m]
    target = [size[0]] + [zero] * N
    for j in range(N):
        one, two = hess[j][j], hess[j + 1][j]
        radius = jnp.sqrt(one * one + two * two)
        cosine, sine = one / radius, two / radius
        top = [cosine * hess[j][i] + sine * hess[j + 1][i] for i in range(N)]
        hess[j + 1] = [cosine * hess[j + 1][i] - sine * hess[j][i] for i in range(N)]
        hess[j] = top
        target[j], target[j + 1] = (
            cosine * target[j] + sine * target[j + 1],
            cosine * target[j + 1] - sine * target[j],
        )
    answer = [None] * N
    for i in reversed(range(N)):
        value = target[i]
        for k in range(i + 1, N):
            value = value - hess[i][k] * answer[k]
        answer[i] = value / hess[i][i]
    for k in range(2):
        total = jnp.zeros((6, 8, 128), F32)
        for i in range(N):
            total = total + (answer[i] / size[i])[None] * d[i, k].reshape(6, 8, 128)
        out_ref[k] = total.reshape(B, 128)

    def drain(n, carry):
        @pl.when(has_up)
        def _():
            send_carry(n).wait_send()
            send_low(n).wait_send()

        @pl.when(has_down)
        def _():
            send_up(n).wait_send()

        for k in range(2):
            @pl.when(has_west)
            def _():
                send_west(n, k).wait_send()

            @pl.when(has_east)
            def _():
                send_east(n, k).wait_send()

        pltpu.make_async_copy(recv1.at[n], recv1.at[n], red1_send.at[n]).wait()
        pltpu.make_async_copy(recv2.at[n], recv2.at[n], red2_send.at[n]).wait()
        return carry

    lax.fori_loop(0, N, drain, 0)


def solution(mesh):
    lines, rows = mesh.shape["line"], mesh.shape["patch"]
    dma = pltpu.SemaphoreType.DMA
    pair = pltpu.VMEM((N, 2, B, 128), F32)
    single = pltpu.VMEM((N, B, 128), F32)
    tile = pltpu.VMEM((N, 8, 128), F32)
    tiles = pltpu.VMEM((N, GROUP - 1, 8, 128), F32)

    def per_device(newton_residual, diag_block, lower, upper, west, east, pivot_inverse):
        arrays = [a.reshape(2, B, B, 128) for a in (pivot_inverse, lower, upper, diag_block, west, east)]
        step = pl.pallas_call(
            functools.partial(kernel, lines, rows),
            out_shape=jax.ShapeDtypeStruct((2, B, 128), F32),
            in_specs=[pl.BlockSpec(memory_space=pl.ANY)] * 7,
            out_specs=pl.BlockSpec(memory_space=pltpu.VMEM),
            scratch_shapes=[
                pltpu.VMEM((6, 2, B, B, 128), jnp.bfloat16),
                pltpu.VMEM((6, 2, B * B, 128), F32),
                pltpu.VMEM((N + 1, 2, B, 128), F32),
                pair, pair, pair, pair,
                single, single, single,
                pair, pair,
                pltpu.VMEM((2, B, 128), F32), pltpu.VMEM((2, B, 128), F32),
                tile, tiles, tile, tiles, tile,
                tile, tile,
                pltpu.VMEM((8, 128), F32),
                dma((7, 2)),
                dma((N,)), dma((N,)), dma((N,)), dma((N,)), dma((N,)), dma((N,)),
                dma((N, 2)), dma((N, 2)), dma((N, 2)), dma((N, 2)),
                dma((N,)), dma((N,)), dma((N,)), dma((N,)),
            ],
            compiler_params=pltpu.CompilerParams(collective_id=0, has_side_effects=True),
        )(newton_residual.reshape(2, B, 128), *arrays)
        return (step * (1.0 / SCALE)).reshape(2, B, 1, 128)

    mats = P("line", None, None, "patch", None)
    return jax.shard_map(
        per_device,
        mesh=mesh,
        in_specs=(P("line", None, "patch", None), mats, mats, mats, mats, mats, mats),
        out_specs=P("line", None, "patch", None),
        check_vma=False,
    )
```

```python
import functools

import jax
import jax.numpy as jnp
from jax import lax
from jax.experimental import pallas as pl
from jax.experimental.pallas import tpu as pltpu
from jax.sharding import PartitionSpec as P

MESH = pl.DeviceIdType.MESH
F32 = jnp.float32
B = 48
N = 4
SCALE = 2.0**-15
PIV, LOW, UP, DIAG, WEST, EAST = range(6)
GROUP = 16
PITCH = 56


def kernel(
    lines, rows,
    r_hbm, piv_hbm, low_hbm, up_hbm, diag_hbm, west_hbm, east_hbm,
    out_ref,
    packed, mats, xin, u, d, z, g, gin, zin, zlow, hw, he, bacc, tmp,
    part1, recv1, part2, recv2, res, gam, coef, eta, over, held, far, mine, loc, col, gsum,
    load_sem, carry_send, carry_recv, up_send, up_recv, low_send, low_recv,
    west_send, west_recv, east_send, east_recv, red1_send, red1_recv, red2_send, red2_recv,
    over_send, over_recv, far_send, far_recv,
):
    y = lax.axis_index("line")
    p = lax.axis_index("patch")
    hbm = (piv_hbm, low_hbm, up_hbm, diag_hbm, west_hbm, east_hbm)

    def load(a, k):
        return pltpu.make_async_copy(hbm[a].at[k], packed.at[a, k], load_sem.at[a, k])

    load_r = pltpu.make_async_copy(r_hbm, tmp, load_sem.at[6, 0])
    load_r.start()
    for a, k in ((PIV, 0), (PIV, 1), (LOW, 1), (LOW, 0), (UP, 1), (UP, 0), (DIAG, 0), (DIAG, 1), (WEST, 1), (EAST, 1), (WEST, 0), (EAST, 0)):
        load(a, k).start()

    x, b = p // GROUP, p % GROUP
    a_me = y * 4 + x

    def peer1(o):
        i = lax.rem(a_me + o, GROUP)
        return (i // 4, (i % 4) * GROUP + b)

    def peer2(o):
        return (y, x * GROUP + lax.rem(b + o, GROUP))

    has_down, has_up = y > 0, y < lines - 1
    has_west, has_east = p > 0, p < rows - 1

    barrier = pltpu.get_barrier_semaphore()
    for o in range(1, GROUP):
        pl.semaphore_signal(barrier, inc=1, device_id=peer1(o), device_id_type=MESH)
        pl.semaphore_signal(barrier, inc=1, device_id=peer2(o), device_id_type=MESH)

    @pl.when(has_west)
    def _():
        pl.semaphore_signal(barrier, inc=1, device_id=(y, p - 1), device_id_type=MESH)

    @pl.when(has_east)
    def _():
        pl.semaphore_signal(barrier, inc=1, device_id=(y, p + 1), device_id_type=MESH)

    u[...] = jnp.zeros_like(u)
    d[...] = jnp.zeros_like(d)
    xin[1:] = jnp.zeros_like(xin[1:])
    part1[...] = jnp.zeros_like(part1)
    coef[...] = jnp.zeros_like(coef)
    eta[...] = jnp.ones_like(eta)
    gam[...] = jnp.ones_like(gam)

    @pl.when(jnp.logical_not(has_west))
    def _():
        hw[...] = jnp.zeros_like(hw)

    @pl.when(jnp.logical_not(has_east))
    def _():
        he[...] = jnp.zeros_like(he)

    @pl.when(jnp.logical_not(has_down))
    def _():
        zlow[...] = jnp.zeros_like(zlow)

    load_r.wait()
    xin[0] = tmp[...] * SCALE

    def widen(a, k):
        pltpu.make_async_copy(packed.at[a, k], packed.at[a, k], load_sem.at[a, k]).wait()

        def body(t, carry):
            for s in range(8):
                i = t * 8 + s
                mats[a, k, pl.ds(i, B, stride=PITCH), :] = packed[a, k, i].astype(F32)
            return carry
        lax.fori_loop(0, B // 8, body, 0)

    def widen_all(first, last):
        def body(t, carry):
            widen(t // 2, t % 2)
            return carry
        lax.fori_loop(first, last, body, 0)

    def block(a, k):
        return mats.at[a, k], PITCH

    def apply(pairs, start=None):
        zero = jnp.zeros((6, 8, 128), F32)
        accs = [zero if start is None else start.reshape(6, 8, 128), zero]
        turn = 0
        for (columns, pitch), v in pairs:
            for j in range(B):
                row = v[pl.ds(j, 8, stride=0), :]
                accs[turn] = accs[turn] + columns[pl.ds(j * pitch, B), :].reshape(6, 8, 128) * row[None]
                turn = 1 - turn
        return (accs[0] + accs[1]).reshape(B, 128)

    def send(src, dst, ssem, rsem, to):
        return pltpu.make_async_remote_copy(
            src_ref=src, dst_ref=dst, send_sem=ssem, recv_sem=rsem, device_id=to, device_id_type=MESH
        )

    def send_carry(n):
        return send(g.at[n, 1], gin.at[n], carry_send.at[n], carry_recv.at[n], (y + 1, p))

    def send_up(n):
        return send(z.at[n, 0], zin.at[n], up_send.at[n], up_recv.at[n], (y - 1, p))

    def send_low(n):
        return send(z.at[n, 1], zlow.at[n], low_send.at[n], low_recv.at[n], (y + 1, p))

    def send_west(n, k):
        return send(z.at[n, k], he.at[n, k], west_send.at[n, k], west_recv.at[n, k], (y, p - 1))

    def send_east(n, k):
        return send(z.at[n, k], hw.at[n, k], east_send.at[n, k], east_recv.at[n, k], (y, p + 1))

    def send_far(n):
        return send(mine.at[n], far.at[n], far_send.at[n], far_recv.at[n], (jnp.where(y == 0, y + 2, y - 2), p))

    order = jnp.where(y == 1, 0, 1)
    coupling = jnp.where(y == 1, LOW, UP)

    def form(first, last):
        def body(j, carry):
            a = apply([((mats.at[PIV, order], PITCH), mats.at[coupling, order, pl.ds(pl.multiple_of(j * PITCH, 8), B)])])
            col[0] = a
            col[1] = apply([((mats.at[coupling, 1 - order], PITCH), col.at[0])])
            over[pl.ds(pl.multiple_of(j * B, 8), B), :] = apply([((mats.at[PIV, 1 - order], PITCH), col.at[1])])
            rows_j = pl.ds(pl.multiple_of(j * B, 8), B)
            send(over.at[rows_j], held.at[rows_j], over_send, over_recv, (jnp.where(y == 1, y - 1, y + 1), p)).start()
            return carry
        lax.fori_loop(first, last, body, 0)

    def down_rest(n, dst):
        tmp[0] = xin[n, 1] - apply([(block(LOW, 1), dst.at[n, 0])])
        dst[n, 1] = apply([(block(PIV, 1), tmp.at[0])])

    def red_start(m):
        q0, q1 = xin[m + 1, 0].reshape(6, 8, 128), xin[m + 1, 1].reshape(6, 8, 128)

        def row(i, a0, a1, b0, b1):
            s = jnp.sum(a0 * b0 + a1 * b1, axis=0)
            part1[m, pl.ds(i, 1), :] = jnp.sum(s, axis=0, keepdims=True)

        for i in range(N):
            row(i, u[i, 0].reshape(6, 8, 128), u[i, 1].reshape(6, 8, 128), q0, q1)
        v0, v1 = u[m, 0].reshape(6, 8, 128), u[m, 1].reshape(6, 8, 128)
        row(4, v0, v1, v0, v1)
        row(5, q0, q1, q0, q1)
        for o in range(1, GROUP):
            send(part1.at[m], recv1.at[m, o - 1], red1_send.at[m], red1_recv.at[m], peer1(o)).start()

    def red_middle(m):
        pltpu.make_async_copy(recv1.at[m], recv1.at[m], red1_recv.at[m]).wait()
        part2[m] = part1[m] + jnp.sum(recv1[m], axis=0)
        for o in range(1, GROUP):
            send(part2.at[m], recv2.at[m, o - 1], red2_send.at[m], red2_recv.at[m], peer2(o)).start()

    def red_end(m):
        pltpu.make_async_copy(recv2.at[m], recv2.at[m], red2_recv.at[m]).wait()
        total = part2[m] + jnp.sum(recv2[m], axis=0)
        res[m] = jnp.broadcast_to(jnp.sum(total, axis=1, keepdims=True), (8, 128))
        gam[m] = res[m, pl.ds(4, 8, stride=0), :]
        for i in range(N):
            value = res[m, pl.ds(i, 8, stride=0), :] / gam[i]
            coef[i] = jnp.where(m >= i, value, 0.0)
        eta[...] = 1.0 / jnp.sqrt(res[m, pl.ds(5, 8, stride=0), :])

    def combined(value, olds):
        total = value.reshape(6, 8, 128)
        for i in range(N):
            total = total - coef[i][None] * olds(i).reshape(6, 8, 128)
        return (total * eta[...][None]).reshape(B, 128)

    inner = jnp.logical_or(y == 1, y == 2)
    outer = jnp.logical_not(inner)

    widen_all(0, 2)
    widen(LOW, 1)

    @pl.when(has_down)
    def _():
        widen(LOW, 0)
        widen_all(4, 12)

    def stage(n, carry):
        later = n > 0

        @pl.when(y == 0)
        def _():
            g[n, 0] = apply([(block(PIV, 0), xin.at[n, 0])])
            down_rest(n, g)

        @pl.when(n == 0)
        def _():
            pl.semaphore_wait(barrier, 2 * (GROUP - 1) + has_west.astype(jnp.int32) + has_east.astype(jnp.int32))

        @pl.when(jnp.logical_and(y == 0, later))
        def _():
            @pl.when(n == 1)
            def _():
                pltpu.make_async_copy(held, held, over_recv).wait()

            mine[n] = apply([((held, B), g.at[n, 1])])
            send_far(n).start()

        @pl.when(y == 0)
        def _():
            send_carry(n).start()

            @pl.when(n == 0)
            def _():
                widen(LOW, 0)
                widen_all(4, 12)

        @pl.when(jnp.logical_and(y == 1, later))
        def _():
            loc[n, 0] = apply([(block(PIV, 0), xin.at[n, 0])])
            down_rest(n, loc)
            send(loc.at[n, 1], gin.at[n], carry_send.at[n], carry_recv.at[n], (y + 1, p)).start()

        @pl.when(later)
        def _():
            red_start(n - 1)

        @pl.when(jnp.logical_and(y == 3, later))
        def _():
            red_middle(n - 1)

        @pl.when(jnp.logical_and(y == 2, n == 0))
        def _():
            form(0, 8)

        @pl.when(has_down)
        def _():
            send_carry(n).wait_recv()

            @pl.when(jnp.logical_and(y == 2, later))
            def _():
                send_far(n).wait_recv()
                gsum[...] = gin[n] + far[n]

            @pl.when(jnp.logical_not(jnp.logical_and(y == 2, later)))
            def _():
                gsum[...] = gin[n]

            tmp[1] = xin[n, 0] - apply([(block(LOW, 0), gsum)])
            g[n, 0] = apply([(block(PIV, 0), tmp.at[1])])
            down_rest(n, g)

        @pl.when(jnp.logical_or(y == 2, jnp.logical_and(y == 1, n == 0)))
        def _():
            send_carry(n).start()

        @pl.when(jnp.logical_and(y == 2, later))
        def _():
            tmp[0] = apply([(block(UP, 0), g.at[n, 1])])
            loc[n, 0] = g[n, 0] - apply([(block(PIV, 0), tmp.at[0])])
            send(loc.at[n, 0], zin.at[n], up_send.at[n], up_recv.at[n], (y - 1, p)).start()

        @pl.when(jnp.logical_and(inner, n == 0))
        def _():
            form(jnp.where(y == 1, 0, 8), jnp.where(y == 1, 36, 24))

        @pl.when(jnp.logical_and(later, has_up))
        def _():
            red_middle(n - 1)

        @pl.when(has_up)
        def _():
            send_up(n).wait_recv()

            @pl.when(jnp.logical_and(y == 1, later))
            def _():
                send_far(n).wait_recv()
                gsum[...] = zin[n] + far[n]

            @pl.when(jnp.logical_not(jnp.logical_and(y == 1, later)))
            def _():
                gsum[...] = zin[n]

            bacc[1] = apply([(block(UP, 1), gsum)])
            z[n, 1] = g[n, 1] - apply([(block(PIV, 1), bacc.at[1])])
            send_low(n).start()

        @pl.when(jnp.logical_not(has_up))
        def _():
            bacc[1] = jnp.zeros((B, 128), F32)
            z[n, 1] = g[n, 1]

        @pl.when(has_west)
        def _():
            send_west(n, 1).start()

        @pl.when(has_east)
        def _():
            send_east(n, 1).start()

        bacc[0] = apply([(block(UP, 0), z.at[n, 1])])
        z[n, 0] = g[n, 0] - apply([(block(PIV, 0), bacc.at[0])])

        @pl.when(jnp.logical_and(y == 3, later))
        def _():
            @pl.when(n == 1)
            def _():
                pltpu.make_async_copy(held, held, over_recv).wait()

            mine[n] = apply([((held, B), z.at[n, 0])])
            send_far(n).start()

        @pl.when(jnp.logical_or(jnp.logical_or(y == 1, y == 3), jnp.logical_and(y == 2, n == 0)))
        def _():
            send_up(n).start()

        @pl.when(has_west)
        def _():
            send_west(n, 0).start()

        @pl.when(has_east)
        def _():
            send_east(n, 0).start()

        @pl.when(jnp.logical_and(inner, n == 0))
        def _():
            form(jnp.where(y == 1, 36, 24), B)

        bacc[1] = apply([(block(DIAG, 1), z.at[n, 1]), (block(LOW, 1), z.at[n, 0])], bacc[1])
        bacc[0] = apply([(block(DIAG, 0), z.at[n, 0])], bacc[0])

        @pl.when(later)
        def _():
            red_end(n - 1)

        for k in range(2):
            u[n, k] = combined(xin[n, k], lambda i: u[i, k])
            d[n, k] = combined(z[n, k], lambda i: d[i, k])

        def halo(k):
            @pl.when(has_west)
            def _():
                send_east(n, k).wait_recv()

            @pl.when(has_east)
            def _():
                send_west(n, k).wait_recv()

        halo(1)
        value = apply([(block(WEST, 1), hw.at[n, 1]), (block(EAST, 1), he.at[n, 1])], bacc[1])
        xin[n + 1, 1] = combined(value, lambda i: xin[i + 1, 1])

        @pl.when(has_down)
        def _():
            send_low(n).wait_recv()
            bacc[0] = apply([(block(LOW, 0), zlow.at[n])], bacc[0])

        halo(0)
        value = apply([(block(WEST, 0), hw.at[n, 0]), (block(EAST, 0), he.at[n, 0])], bacc[0])
        xin[n + 1, 0] = combined(value, lambda i: xin[i + 1, 0])
        return carry

    lax.fori_loop(0, N, stage, 0)
    red_start(N - 1)
    red_middle(N - 1)
    red_end(N - 1)

    size = [jnp.sqrt(gam[i]) for i in range(N)]
    zero = jnp.zeros((8, 128), F32)

    def entry(m, i):
        return res[m, pl.ds(i, 8, stride=0), :]

    hess = [[zero] * N for _ in range(N + 1)]
    for m in range(N):
        for i in range(m + 1):
            hess[i][m] = entry(m, i) / (size[i] * size[m])
        if m < N - 1:
            hess[m + 1][m] = size[m + 1] * jnp.sqrt(entry(m, 5)) / size[m]
        else:
            rest = entry(m, 5)
            for i in range(N):
                rest = rest - entry(m, i) * entry(m, i) / gam[i]
            hess[N][m] = jnp.sqrt(jnp.maximum(rest, 0.0)) / size[m]
    target = [size[0]] + [zero] * N
    for j in range(N):
        one, two = hess[j][j], hess[j + 1][j]
        radius = jnp.sqrt(one * one + two * two)
        cosine, sine = one / radius, two / radius
        top = [cosine * hess[j][i] + sine * hess[j + 1][i] for i in range(N)]
        hess[j + 1] = [cosine * hess[j + 1][i] - sine * hess[j][i] for i in range(N)]
        hess[j] = top
        target[j], target[j + 1] = (
            cosine * target[j] + sine * target[j + 1],
            cosine * target[j + 1] - sine * target[j],
        )
    answer = [None] * N
    for i in reversed(range(N)):
        value = target[i]
        for k in range(i + 1, N):
            value = value - hess[i][k] * answer[k]
        answer[i] = value / hess[i][i]
    for k in range(2):
        total = jnp.zeros((6, 8, 128), F32)
        for i in range(N):
            total = total + (answer[i] / size[i])[None] * d[i, k].reshape(6, 8, 128)
        out_ref[k] = total.reshape(B, 128)

    def drain(n, carry):
        @pl.when(has_up)
        def _():
            send_carry(n).wait_send()
            send_low(n).wait_send()

        @pl.when(has_down)
        def _():
            send_up(n).wait_send()

        for k in range(2):
            @pl.when(has_west)
            def _():
                send_west(n, k).wait_send()

            @pl.when(has_east)
            def _():
                send_east(n, k).wait_send()

        @pl.when(jnp.logical_and(outer, n > 0))
        def _():
            send_far(n).wait_send()

        pltpu.make_async_copy(recv1.at[n], recv1.at[n], red1_send.at[n]).wait()
        pltpu.make_async_copy(recv2.at[n], recv2.at[n], red2_send.at[n]).wait()
        return carry

    lax.fori_loop(0, N, drain, 0)

    @pl.when(inner)
    def _():
        pltpu.make_async_copy(over, over, over_send).wait()


def solution(mesh):
    lines, rows = mesh.shape["line"], mesh.shape["patch"]
    dma = pltpu.SemaphoreType.DMA
    pair = pltpu.VMEM((N, 2, B, 128), F32)
    single = pltpu.VMEM((N, B, 128), F32)
    tile = pltpu.VMEM((N, 8, 128), F32)
    tiles = pltpu.VMEM((N, GROUP - 1, 8, 128), F32)

    def per_device(newton_residual, diag_block, lower, upper, west, east, pivot_inverse):
        arrays = [a.reshape(2, B, B, 128) for a in (pivot_inverse, lower, upper, diag_block, west, east)]
        step = pl.pallas_call(
            functools.partial(kernel, lines, rows),
            out_shape=jax.ShapeDtypeStruct((2, B, 128), F32),
            in_specs=[pl.BlockSpec(memory_space=pl.ANY)] * 7,
            out_specs=pl.BlockSpec(memory_space=pltpu.VMEM),
            scratch_shapes=[
                pltpu.VMEM((6, 2, B, B, 128), jnp.bfloat16),
                pltpu.VMEM((6, 2, B * PITCH, 128), F32),
                pltpu.VMEM((N + 1, 2, B, 128), F32),
                pair, pair, pair, pair,
                single, single, single,
                pair, pair,
                pltpu.VMEM((2, B, 128), F32), pltpu.VMEM((2, B, 128), F32),
                tile, tiles, tile, tiles, tile,
                tile, tile,
                pltpu.VMEM((8, 128), F32),
                pltpu.VMEM((B * B, 128), F32), pltpu.VMEM((B * B, 128), F32),
                single, single, pair,
                pltpu.VMEM((2, B, 128), F32), pltpu.VMEM((B, 128), F32),
                dma((7, 2)),
                dma((N,)), dma((N,)), dma((N,)), dma((N,)), dma((N,)), dma((N,)),
                dma((N, 2)), dma((N, 2)), dma((N, 2)), dma((N, 2)),
                dma((N,)), dma((N,)), dma((N,)), dma((N,)),
                dma, dma, dma((N,)), dma((N,)),
            ],
            compiler_params=pltpu.CompilerParams(collective_id=0, has_side_effects=True),
        )(newton_residual.reshape(2, B, 128), *arrays)
        return (step * (1.0 / SCALE)).reshape(2, B, 1, 128)

    mats = P("line", None, None, "patch", None)
    return jax.shard_map(
        per_device,
        mesh=mesh,
        in_specs=(P("line", None, "patch", None), mats, mats, mats, mats, mats, mats),
        out_specs=P("line", None, "patch", None),
        check_vma=False,
    )
```

```python
import functools

import jax
import jax.numpy as jnp
from jax import lax
from jax.experimental import pallas as pl
from jax.experimental.pallas import tpu as pltpu
from jax.sharding import PartitionSpec as P

MESH = pl.DeviceIdType.MESH
F32 = jnp.float32
B = 48
N = 4
SCALE = 2.0**-15
PIV, LOW, UP, DIAG, WEST, EAST = range(6)
GROUP = 16
PITCH = 56


def kernel(
    lines, rows,
    r_hbm, piv_hbm, low_hbm, up_hbm, diag_hbm, west_hbm, east_hbm,
    out_ref,
    packed, mats, xin, u, d, z, g, gin, zin, zlow, hw, he, bacc, tmp,
    part1, recv1, part2, recv2, res, gam, coef, eta, over, held, far, mine, loc, col, gsum,
    load_sem, carry_send, carry_recv, up_send, up_recv, low_send, low_recv,
    west_send, west_recv, east_send, east_recv, red1_send, red1_recv, red2_send, red2_recv,
    over_send, over_recv, far_send, far_recv,
):
    y = lax.axis_index("line")
    p = lax.axis_index("patch")
    hbm = (piv_hbm, low_hbm, up_hbm, diag_hbm, west_hbm, east_hbm)

    def load(a, k):
        return pltpu.make_async_copy(hbm[a].at[k], packed.at[a, k], load_sem.at[a, k])

    load_r = pltpu.make_async_copy(r_hbm, tmp, load_sem.at[6, 0])
    load_r.start()
    for a, k in ((PIV, 0), (PIV, 1), (LOW, 1), (LOW, 0), (UP, 1), (UP, 0), (DIAG, 0), (DIAG, 1), (WEST, 1), (EAST, 1), (WEST, 0), (EAST, 0)):
        load(a, k).start()

    x, b = p // GROUP, p % GROUP
    a_me = y * 4 + x

    def peer1(o):
        i = lax.rem(a_me + o, GROUP)
        return (i // 4, (i % 4) * GROUP + b)

    def peer2(o):
        return (y, x * GROUP + lax.rem(b + o, GROUP))

    has_down, has_up = y > 0, y < lines - 1
    has_west, has_east = p > 0, p < rows - 1

    barrier = pltpu.get_barrier_semaphore()
    for o in range(1, GROUP):
        pl.semaphore_signal(barrier, inc=1, device_id=peer1(o), device_id_type=MESH)
        pl.semaphore_signal(barrier, inc=1, device_id=peer2(o), device_id_type=MESH)

    @pl.when(has_west)
    def _():
        pl.semaphore_signal(barrier, inc=1, device_id=(y, p - 1), device_id_type=MESH)

    @pl.when(has_east)
    def _():
        pl.semaphore_signal(barrier, inc=1, device_id=(y, p + 1), device_id_type=MESH)

    u[...] = jnp.zeros_like(u)
    d[...] = jnp.zeros_like(d)
    xin[1:] = jnp.zeros_like(xin[1:])
    part1[...] = jnp.zeros_like(part1)
    coef[...] = jnp.zeros_like(coef)
    eta[...] = jnp.ones_like(eta)
    gam[...] = jnp.ones_like(gam)

    @pl.when(jnp.logical_not(has_west))
    def _():
        hw[...] = jnp.zeros_like(hw)

    @pl.when(jnp.logical_not(has_east))
    def _():
        he[...] = jnp.zeros_like(he)

    @pl.when(jnp.logical_not(has_down))
    def _():
        zlow[...] = jnp.zeros_like(zlow)

    load_r.wait()
    xin[0] = tmp[...] * SCALE

    def widen(a, k):
        pltpu.make_async_copy(packed.at[a, k], packed.at[a, k], load_sem.at[a, k]).wait()

        def body(t, carry):
            for s in range(8):
                i = t * 8 + s
                mats[a, k, pl.ds(i, B, stride=PITCH), :] = packed[a, k, i].astype(F32)
            return carry
        lax.fori_loop(0, B // 8, body, 0)

    def widen_all(first, last):
        def body(t, carry):
            widen(t // 2, t % 2)
            return carry
        lax.fori_loop(first, last, body, 0)

    def block(a, k):
        return mats.at[a, k], PITCH

    def apply(pairs, start=None):
        zero = jnp.zeros((6, 8, 128), F32)
        accs = [zero if start is None else start.reshape(6, 8, 128), zero]
        turn = 0
        for (columns, pitch), v in pairs:
            for j in range(B):
                row = v[pl.ds(j, 8, stride=0), :]
                accs[turn] = accs[turn] + columns[pl.ds(j * pitch, B), :].reshape(6, 8, 128) * row[None]
                turn = 1 - turn
        return (accs[0] + accs[1]).reshape(B, 128)

    def send(src, dst, ssem, rsem, to):
        return pltpu.make_async_remote_copy(
            src_ref=src, dst_ref=dst, send_sem=ssem, recv_sem=rsem, device_id=to, device_id_type=MESH
        )

    def send_carry(n):
        return send(g.at[n, 1], gin.at[n], carry_send.at[n], carry_recv.at[n], (y + 1, p))

    def send_up(n):
        return send(z.at[n, 0], zin.at[n], up_send.at[n], up_recv.at[n], (y - 1, p))

    def send_low(n):
        return send(z.at[n, 1], zlow.at[n], low_send.at[n], low_recv.at[n], (y + 1, p))

    def send_west(n, k):
        return send(z.at[n, k], he.at[n, k], west_send.at[n, k], west_recv.at[n, k], (y, p - 1))

    def send_east(n, k):
        return send(z.at[n, k], hw.at[n, k], east_send.at[n, k], east_recv.at[n, k], (y, p + 1))

    def send_far(n):
        return send(mine.at[n], far.at[n], far_send.at[n], far_recv.at[n], (y + 2, p))

    def post(j):
        rows_j = pl.ds(pl.multiple_of(j * B, 8), B)
        send(over.at[rows_j], held.at[rows_j], over_send, over_recv, (y - 1, p)).start()

    def post_all(first, last):
        def body(j, carry):
            post(j)
            return carry
        lax.fori_loop(first, last, body, 0)

    def form(first, last, end):
        def body(j, carry):
            rows_j = pl.ds(pl.multiple_of(j * B, 8), B)
            col[0] = apply([(block(PIV, 0), mats.at[LOW, 0, pl.ds(pl.multiple_of(j * PITCH, 8), B)])])
            col[1] = apply([(block(LOW, 1), col.at[0])])
            col[2] = apply([(block(PIV, 1), col.at[1])])

            @pl.when(y == 1)
            def _():
                over[rows_j, :] = col[2]

            @pl.when(y == 3)
            def _():
                col[1] = apply([(block(UP, 0), col.at[2])])
                over[rows_j, :] = -col[0] - apply([(block(PIV, 0), col.at[1])])

            @pl.when(j < end)
            def _():
                post(j)
            return carry
        lax.fori_loop(first, last, body, 0)

    def down_rest(n, dst):
        tmp[0] = xin[n, 1] - apply([(block(LOW, 1), dst.at[n, 0])])
        dst[n, 1] = apply([(block(PIV, 1), tmp.at[0])])

    def red_start(m):
        q0, q1 = xin[m + 1, 0].reshape(6, 8, 128), xin[m + 1, 1].reshape(6, 8, 128)

        def row(i, a0, a1, b0, b1):
            s = jnp.sum(a0 * b0 + a1 * b1, axis=0)
            part1[m, pl.ds(i, 1), :] = jnp.sum(s, axis=0, keepdims=True)

        for i in range(N):
            row(i, u[i, 0].reshape(6, 8, 128), u[i, 1].reshape(6, 8, 128), q0, q1)
        v0, v1 = u[m, 0].reshape(6, 8, 128), u[m, 1].reshape(6, 8, 128)
        row(4, v0, v1, v0, v1)
        row(5, q0, q1, q0, q1)
        for o in range(1, GROUP):
            send(part1.at[m], recv1.at[m, o - 1], red1_send.at[m], red1_recv.at[m], peer1(o)).start()

    def red_middle(m):
        pltpu.make_async_copy(recv1.at[m], recv1.at[m], red1_recv.at[m]).wait()
        part2[m] = part1[m] + jnp.sum(recv1[m], axis=0)
        for o in range(1, GROUP):
            send(part2.at[m], recv2.at[m, o - 1], red2_send.at[m], red2_recv.at[m], peer2(o)).start()

    def red_end(m):
        pltpu.make_async_copy(recv2.at[m], recv2.at[m], red2_recv.at[m]).wait()
        total = part2[m] + jnp.sum(recv2[m], axis=0)
        res[m] = jnp.broadcast_to(jnp.sum(total, axis=1, keepdims=True), (8, 128))
        gam[m] = res[m, pl.ds(4, 8, stride=0), :]
        for i in range(N):
            value = res[m, pl.ds(i, 8, stride=0), :] / gam[i]
            coef[i] = jnp.where(m >= i, value, 0.0)
        eta[...] = 1.0 / jnp.sqrt(res[m, pl.ds(5, 8, stride=0), :])

    def combined(value, olds):
        total = value.reshape(6, 8, 128)
        for i in range(N):
            total = total - coef[i][None] * olds(i).reshape(6, 8, 128)
        return (total * eta[...][None]).reshape(B, 128)

    forms = jnp.logical_or(y == 1, y == 3)

    widen_all(0, 2)
    widen(LOW, 1)

    @pl.when(has_down)
    def _():
        widen(LOW, 0)
        widen_all(4, 12)

    def stage(n, carry):
        later = n > 0
        down_short = n > 1

        @pl.when(y == 0)
        def _():
            g[n, 0] = apply([(block(PIV, 0), xin.at[n, 0])])
            down_rest(n, g)

        @pl.when(n == 0)
        def _():
            pl.semaphore_wait(barrier, 2 * (GROUP - 1) + has_west.astype(jnp.int32) + has_east.astype(jnp.int32))

        @pl.when(jnp.logical_and(y == 0, down_short))
        def _():
            @pl.when(n == 2)
            def _():
                pltpu.make_async_copy(held, held, over_recv).wait()

            mine[n] = apply([((held, B), g.at[n, 1])])
            send_far(n).start()

        @pl.when(y == 0)
        def _():
            send_carry(n).start()

            @pl.when(n == 0)
            def _():
                widen(LOW, 0)
                widen_all(4, 12)

        @pl.when(jnp.logical_and(y == 1, down_short))
        def _():
            loc[n, 0] = apply([(block(PIV, 0), xin.at[n, 0])])
            down_rest(n, loc)
            send(loc.at[n, 1], gin.at[n], carry_send.at[n], carry_recv.at[n], (y + 1, p)).start()

        @pl.when(later)
        def _():
            red_start(n - 1)

        @pl.when(jnp.logical_and(y == 3, later))
        def _():
            loc[n, 0] = apply([(block(PIV, 0), xin.at[n, 0])])
            down_rest(n, loc)
            tmp[0] = apply([(block(UP, 0), loc.at[n, 1])])
            mine[n] = loc[n, 0] - apply([(block(PIV, 0), tmp.at[0])])
            send(mine.at[n], zin.at[n], up_send.at[n], up_recv.at[n], (y - 1, p)).start()
            red_middle(n - 1)

        @pl.when(jnp.logical_and(y == 3, n == 0))
        def _():
            form(0, 22, 18)

        @pl.when(has_down)
        def _():
            send_carry(n).wait_recv()

            @pl.when(jnp.logical_and(y == 2, down_short))
            def _():
                send_far(n).wait_recv()
                gsum[...] = gin[n] + far[n]

            @pl.when(jnp.logical_not(jnp.logical_and(y == 2, down_short)))
            def _():
                gsum[...] = gin[n]

            tmp[1] = xin[n, 0] - apply([(block(LOW, 0), gsum)])
            g[n, 0] = apply([(block(PIV, 0), tmp.at[1])])
            down_rest(n, g)

        @pl.when(jnp.logical_or(y == 2, jnp.logical_and(y == 1, jnp.logical_not(down_short))))
        def _():
            send_carry(n).start()

        @pl.when(jnp.logical_and(y == 1, n == 0))
        def _():
            form(0, 36, 16)

        @pl.when(jnp.logical_and(later, y < 2))
        def _():
            red_middle(n - 1)

        @pl.when(has_up)
        def _():
            send_up(n).wait_recv()

            @pl.when(jnp.logical_and(y == 2, later))
            def _():
                @pl.when(n == 1)
                def _():
                    pltpu.make_async_copy(held, held, over_recv).wait()

                gsum[...] = apply([((held, B), g.at[n, 1])], zin[n])

            @pl.when(jnp.logical_not(jnp.logical_and(y == 2, later)))
            def _():
                gsum[...] = zin[n]

            bacc[1] = apply([(block(UP, 1), gsum)])
            z[n, 1] = g[n, 1] - apply([(block(PIV, 1), bacc.at[1])])
            send_low(n).start()

        @pl.when(jnp.logical_not(has_up))
        def _():
            bacc[1] = jnp.zeros((B, 128), F32)
            z[n, 1] = g[n, 1]

        @pl.when(has_west)
        def _():
            send_west(n, 1).start()

        @pl.when(has_east)
        def _():
            send_east(n, 1).start()

        bacc[0] = apply([(block(UP, 0), z.at[n, 1])])
        z[n, 0] = g[n, 0] - apply([(block(PIV, 0), bacc.at[0])])

        @pl.when(jnp.logical_or(jnp.logical_or(y == 1, y == 2), jnp.logical_and(y == 3, n == 0)))
        def _():
            send_up(n).start()

        @pl.when(has_west)
        def _():
            send_west(n, 0).start()

        @pl.when(has_east)
        def _():
            send_east(n, 0).start()

        @pl.when(jnp.logical_and(y == 2, later))
        def _():
            red_middle(n - 1)

        @pl.when(jnp.logical_and(forms, n == 0))
        def _():
            post_all(jnp.where(y == 1, 16, 18), jnp.where(y == 1, 36, 22))
            form(jnp.where(y == 1, 36, 22), B, B)

        bacc[1] = apply([(block(DIAG, 1), z.at[n, 1]), (block(LOW, 1), z.at[n, 0])], bacc[1])
        bacc[0] = apply([(block(DIAG, 0), z.at[n, 0])], bacc[0])

        @pl.when(later)
        def _():
            red_end(n - 1)

        for k in range(2):
            u[n, k] = combined(xin[n, k], lambda i: u[i, k])
            d[n, k] = combined(z[n, k], lambda i: d[i, k])

        def halo(k):
            @pl.when(has_west)
            def _():
                send_east(n, k).wait_recv()

            @pl.when(has_east)
            def _():
                send_west(n, k).wait_recv()

        halo(1)
        value = apply([(block(WEST, 1), hw.at[n, 1]), (block(EAST, 1), he.at[n, 1])], bacc[1])
        xin[n + 1, 1] = combined(value, lambda i: xin[i + 1, 1])

        @pl.when(has_down)
        def _():
            send_low(n).wait_recv()
            bacc[0] = apply([(block(LOW, 0), zlow.at[n])], bacc[0])

        halo(0)
        value = apply([(block(WEST, 0), hw.at[n, 0]), (block(EAST, 0), he.at[n, 0])], bacc[0])
        xin[n + 1, 0] = combined(value, lambda i: xin[i + 1, 0])
        return carry

    lax.fori_loop(0, N, stage, 0)
    red_start(N - 1)
    red_middle(N - 1)
    red_end(N - 1)

    size = [jnp.sqrt(gam[i]) for i in range(N)]
    zero = jnp.zeros((8, 128), F32)

    def entry(m, i):
        return res[m, pl.ds(i, 8, stride=0), :]

    hess = [[zero] * N for _ in range(N + 1)]
    for m in range(N):
        for i in range(m + 1):
            hess[i][m] = entry(m, i) / (size[i] * size[m])
        if m < N - 1:
            hess[m + 1][m] = size[m + 1] * jnp.sqrt(entry(m, 5)) / size[m]
        else:
            rest = entry(m, 5)
            for i in range(N):
                rest = rest - entry(m, i) * entry(m, i) / gam[i]
            hess[N][m] = jnp.sqrt(jnp.maximum(rest, 0.0)) / size[m]
    target = [size[0]] + [zero] * N
    for j in range(N):
        one, two = hess[j][j], hess[j + 1][j]
        radius = jnp.sqrt(one * one + two * two)
        cosine, sine = one / radius, two / radius
        top = [cosine * hess[j][i] + sine * hess[j + 1][i] for i in range(N)]
        hess[j + 1] = [cosine * hess[j + 1][i] - sine * hess[j][i] for i in range(N)]
        hess[j] = top
        target[j], target[j + 1] = (
            cosine * target[j] + sine * target[j + 1],
            cosine * target[j + 1] - sine * target[j],
        )
    answer = [None] * N
    for i in reversed(range(N)):
        value = target[i]
        for k in range(i + 1, N):
            value = value - hess[i][k] * answer[k]
        answer[i] = value / hess[i][i]
    for k in range(2):
        total = jnp.zeros((6, 8, 128), F32)
        for i in range(N):
            total = total + (answer[i] / size[i])[None] * d[i, k].reshape(6, 8, 128)
        out_ref[k] = total.reshape(B, 128)

    def drain(n, carry):
        @pl.when(has_up)
        def _():
            send_carry(n).wait_send()
            send_low(n).wait_send()

        @pl.when(has_down)
        def _():
            send_up(n).wait_send()

        for k in range(2):
            @pl.when(has_west)
            def _():
                send_west(n, k).wait_send()

            @pl.when(has_east)
            def _():
                send_east(n, k).wait_send()

        @pl.when(jnp.logical_and(y == 0, n > 1))
        def _():
            send_far(n).wait_send()

        pltpu.make_async_copy(recv1.at[n], recv1.at[n], red1_send.at[n]).wait()
        pltpu.make_async_copy(recv2.at[n], recv2.at[n], red2_send.at[n]).wait()
        return carry

    lax.fori_loop(0, N, drain, 0)

    @pl.when(forms)
    def _():
        pltpu.make_async_copy(over, over, over_send).wait()


def solution(mesh):
    lines, rows = mesh.shape["line"], mesh.shape["patch"]
    dma = pltpu.SemaphoreType.DMA
    pair = pltpu.VMEM((N, 2, B, 128), F32)
    single = pltpu.VMEM((N, B, 128), F32)
    tile = pltpu.VMEM((N, 8, 128), F32)
    tiles = pltpu.VMEM((N, GROUP - 1, 8, 128), F32)

    def per_device(newton_residual, diag_block, lower, upper, west, east, pivot_inverse):
        arrays = [a.reshape(2, B, B, 128) for a in (pivot_inverse, lower, upper, diag_block, west, east)]
        step = pl.pallas_call(
            functools.partial(kernel, lines, rows),
            out_shape=jax.ShapeDtypeStruct((2, B, 128), F32),
            in_specs=[pl.BlockSpec(memory_space=pl.ANY)] * 7,
            out_specs=pl.BlockSpec(memory_space=pltpu.VMEM),
            scratch_shapes=[
                pltpu.VMEM((6, 2, B, B, 128), jnp.bfloat16),
                pltpu.VMEM((6, 2, B * PITCH, 128), F32),
                pltpu.VMEM((N + 1, 2, B, 128), F32),
                pair, pair, pair, pair,
                single, single, single,
                pair, pair,
                pltpu.VMEM((2, B, 128), F32), pltpu.VMEM((2, B, 128), F32),
                tile, tiles, tile, tiles, tile,
                tile, tile,
                pltpu.VMEM((8, 128), F32),
                pltpu.VMEM((B * B, 128), F32), pltpu.VMEM((B * B, 128), F32),
                single, single, pair,
                pltpu.VMEM((3, B, 128), F32), pltpu.VMEM((B, 128), F32),
                dma((7, 2)),
                dma((N,)), dma((N,)), dma((N,)), dma((N,)), dma((N,)), dma((N,)),
                dma((N, 2)), dma((N, 2)), dma((N, 2)), dma((N, 2)),
                dma((N,)), dma((N,)), dma((N,)), dma((N,)),
                dma, dma, dma((N,)), dma((N,)),
            ],
            compiler_params=pltpu.CompilerParams(collective_id=0, has_side_effects=True),
        )(newton_residual.reshape(2, B, 128), *arrays)
        return (step * (1.0 / SCALE)).reshape(2, B, 1, 128)

    mats = P("line", None, None, "patch", None)
    return jax.shard_map(
        per_device,
        mesh=mesh,
        in_specs=(P("line", None, "patch", None), mats, mats, mats, mats, mats, mats),
        out_specs=P("line", None, "patch", None),
        check_vma=False,
    )
```

```python
import functools

import jax
import jax.numpy as jnp
from jax import lax
from jax.experimental import pallas as pl
from jax.experimental.pallas import tpu as pltpu
from jax.sharding import PartitionSpec as P

MESH = pl.DeviceIdType.MESH
F32 = jnp.float32
B = 48
N = 4
SCALE = 2.0**-15
PIV, LOW, UP, DIAG, WEST, EAST = range(6)
GROUP = 16
PITCH = 56


def kernel(
    lines, rows,
    r_hbm, piv_hbm, low_hbm, up_hbm, diag_hbm, west_hbm, east_hbm,
    out_ref,
    packed, mats, xin, u, d, z, g, gin, zin, zlow, hw, he, bacc, tmp,
    part1, recv1, part2, recv2, res, gam, coef, eta, over, held, far, mine, loc, col, gsum,
    load_sem, carry_send, carry_recv, up_send, up_recv, low_send, low_recv,
    west_send, west_recv, east_send, east_recv, red1_send, red1_recv, red2_send, red2_recv,
    over_send, over_recv, far_send, far_recv,
):
    y = lax.axis_index("line")
    p = lax.axis_index("patch")
    hbm = (piv_hbm, low_hbm, up_hbm, diag_hbm, west_hbm, east_hbm)

    def load(a, k):
        return pltpu.make_async_copy(hbm[a].at[k], packed.at[a, k], load_sem.at[a, k])

    load_r = pltpu.make_async_copy(r_hbm, tmp, load_sem.at[6, 0])
    load_r.start()
    for a, k in ((PIV, 0), (PIV, 1), (LOW, 1), (LOW, 0), (UP, 1), (UP, 0), (DIAG, 0), (DIAG, 1), (WEST, 1), (EAST, 1), (WEST, 0), (EAST, 0)):
        load(a, k).start()

    x, b = p // GROUP, p % GROUP
    a_me = y * 4 + x

    def peer1(o):
        i = lax.rem(a_me + o, GROUP)
        return (i // 4, (i % 4) * GROUP + b)

    def peer2(o):
        return (y, x * GROUP + lax.rem(b + o, GROUP))

    has_down, has_up = y > 0, y < lines - 1
    has_west, has_east = p > 0, p < rows - 1

    barrier = pltpu.get_barrier_semaphore()
    for o in range(1, GROUP):
        pl.semaphore_signal(barrier, inc=1, device_id=peer1(o), device_id_type=MESH)
        pl.semaphore_signal(barrier, inc=1, device_id=peer2(o), device_id_type=MESH)

    @pl.when(has_west)
    def _():
        pl.semaphore_signal(barrier, inc=1, device_id=(y, p - 1), device_id_type=MESH)

    @pl.when(has_east)
    def _():
        pl.semaphore_signal(barrier, inc=1, device_id=(y, p + 1), device_id_type=MESH)

    u[...] = jnp.zeros_like(u)
    d[...] = jnp.zeros_like(d)
    xin[1:] = jnp.zeros_like(xin[1:])
    part1[...] = jnp.zeros_like(part1)
    coef[...] = jnp.zeros_like(coef)
    eta[...] = jnp.ones_like(eta)
    gam[...] = jnp.ones_like(gam)

    @pl.when(jnp.logical_not(has_west))
    def _():
        hw[...] = jnp.zeros_like(hw)

    @pl.when(jnp.logical_not(has_east))
    def _():
        he[...] = jnp.zeros_like(he)

    @pl.when(jnp.logical_not(has_down))
    def _():
        zlow[...] = jnp.zeros_like(zlow)

    load_r.wait()
    xin[0] = tmp[...] * SCALE

    def widen(a, k):
        pltpu.make_async_copy(packed.at[a, k], packed.at[a, k], load_sem.at[a, k]).wait()

        def body(t, carry):
            for s in range(8):
                i = t * 8 + s
                mats[a, k, pl.ds(i, B, stride=PITCH), :] = packed[a, k, i].astype(F32)
            return carry
        lax.fori_loop(0, B // 8, body, 0)

    def widen_all(first, last):
        def body(t, carry):
            widen(t // 2, t % 2)
            return carry
        lax.fori_loop(first, last, body, 0)

    def block(a, k):
        return mats.at[a, k], PITCH

    def apply(pairs, start=None):
        zero = jnp.zeros((6, 8, 128), F32)
        accs = [zero if start is None else start.reshape(6, 8, 128), zero]
        turn = 0
        for (columns, pitch), v in pairs:
            for j in range(B):
                row = v[pl.ds(j, 8, stride=0), :]
                accs[turn] = accs[turn] + columns[pl.ds(j * pitch, B), :].reshape(6, 8, 128) * row[None]
                turn = 1 - turn
        return (accs[0] + accs[1]).reshape(B, 128)

    def send(src, dst, ssem, rsem, to):
        return pltpu.make_async_remote_copy(
            src_ref=src, dst_ref=dst, send_sem=ssem, recv_sem=rsem, device_id=to, device_id_type=MESH
        )

    def send_carry(n):
        return send(g.at[n, 1], gin.at[n], carry_send.at[n], carry_recv.at[n], (y + 1, p))

    def send_up(n):
        return send(z.at[n, 0], zin.at[n], up_send.at[n], up_recv.at[n], (y - 1, p))

    def send_low(n):
        return send(z.at[n, 1], zlow.at[n], low_send.at[n], low_recv.at[n], (y + 1, p))

    def send_west(n, k):
        return send(z.at[n, k], he.at[n, k], west_send.at[n, k], west_recv.at[n, k], (y, p - 1))

    def send_east(n, k):
        return send(z.at[n, k], hw.at[n, k], east_send.at[n, k], east_recv.at[n, k], (y, p + 1))

    def send_far(n):
        return send(mine.at[n], far.at[n], far_send.at[n], far_recv.at[n], (y + 2, p))

    def post(j):
        rows_j = pl.ds(pl.multiple_of(j * B, 8), B)
        send(over.at[rows_j], held.at[rows_j], over_send, over_recv, (y - 1, p)).start()

    def post_all(first, last):
        def body(j, carry):
            post(j)
            return carry
        lax.fori_loop(first, last, body, 0)

    def form(first, last, end):
        def body(j, carry):
            rows_j = pl.ds(pl.multiple_of(j * B, 8), B)
            col[0] = apply([(block(PIV, 0), mats.at[LOW, 0, pl.ds(pl.multiple_of(j * PITCH, 8), B)])])
            col[1] = apply([(block(LOW, 1), col.at[0])])
            col[2] = apply([(block(PIV, 1), col.at[1])])

            @pl.when(y == 1)
            def _():
                over[rows_j, :] = col[2]

            @pl.when(y == 3)
            def _():
                col[1] = apply([(block(UP, 0), col.at[2])])
                over[rows_j, :] = -col[0] - apply([(block(PIV, 0), col.at[1])])

            @pl.when(j < end)
            def _():
                post(j)
            return carry
        lax.fori_loop(first, last, body, 0)

    def down_rest(n, dst):
        tmp[0] = xin[n, 1] - apply([(block(LOW, 1), dst.at[n, 0])])
        dst[n, 1] = apply([(block(PIV, 1), tmp.at[0])])

    def red_start(m):
        q0, q1 = xin[m + 1, 0].reshape(6, 8, 128), xin[m + 1, 1].reshape(6, 8, 128)

        def row(i, a0, a1, b0, b1):
            s = jnp.sum(a0 * b0 + a1 * b1, axis=0)
            part1[m, pl.ds(i, 1), :] = jnp.sum(s, axis=0, keepdims=True)

        for i in range(N):
            row(i, u[i, 0].reshape(6, 8, 128), u[i, 1].reshape(6, 8, 128), q0, q1)
        v0, v1 = u[m, 0].reshape(6, 8, 128), u[m, 1].reshape(6, 8, 128)
        row(4, v0, v1, v0, v1)
        row(5, q0, q1, q0, q1)
        for o in range(1, GROUP):
            send(part1.at[m], recv1.at[m, o - 1], red1_send.at[m], red1_recv.at[m], peer1(o)).start()

    def red_middle(m):
        pltpu.make_async_copy(recv1.at[m], recv1.at[m], red1_recv.at[m]).wait()
        part2[m] = part1[m] + jnp.sum(recv1[m], axis=0)
        for o in range(1, GROUP):
            send(part2.at[m], recv2.at[m, o - 1], red2_send.at[m], red2_recv.at[m], peer2(o)).start()

    def red_end(m):
        pltpu.make_async_copy(recv2.at[m], recv2.at[m], red2_recv.at[m]).wait()
        total = part2[m] + jnp.sum(recv2[m], axis=0)
        res[m] = jnp.broadcast_to(jnp.sum(total, axis=1, keepdims=True), (8, 128))
        gam[m] = res[m, pl.ds(4, 8, stride=0), :]
        for i in range(N):
            value = res[m, pl.ds(i, 8, stride=0), :] / gam[i]
            coef[i] = jnp.where(m >= i, value, 0.0)
        eta[...] = 1.0 / jnp.sqrt(res[m, pl.ds(5, 8, stride=0), :])

    def combined(value, olds):
        total = value.reshape(6, 8, 128)
        for i in range(N):
            total = total - coef[i][None] * olds(i).reshape(6, 8, 128)
        return (total * eta[...][None]).reshape(B, 128)

    forms = jnp.logical_or(y == 1, y == 3)

    widen_all(0, 2)
    widen(LOW, 1)

    @pl.when(has_down)
    def _():
        widen(LOW, 0)
        widen_all(4, 12)

    def stage(n, carry):
        later = n > 0
        down_short = n > 1

        @pl.when(y == 0)
        def _():
            g[n, 0] = apply([(block(PIV, 0), xin.at[n, 0])])
            down_rest(n, g)

        @pl.when(n == 0)
        def _():
            pl.semaphore_wait(barrier, 2 * (GROUP - 1) + has_west.astype(jnp.int32) + has_east.astype(jnp.int32))

        @pl.when(jnp.logical_and(y == 0, down_short))
        def _():
            @pl.when(n == 2)
            def _():
                pltpu.make_async_copy(held, held, over_recv).wait()

            mine[n] = apply([((held, B), g.at[n, 1])])
            send_far(n).start()

        @pl.when(y == 0)
        def _():
            send_carry(n).start()

            @pl.when(n == 0)
            def _():
                widen(LOW, 0)
                widen_all(4, 12)

        @pl.when(jnp.logical_and(y == 1, down_short))
        def _():
            loc[n, 0] = apply([(block(PIV, 0), xin.at[n, 0])])
            down_rest(n, loc)
            send(loc.at[n, 1], gin.at[n], carry_send.at[n], carry_recv.at[n], (y + 1, p)).start()

        @pl.when(later)
        def _():
            red_start(n - 1)

        @pl.when(jnp.logical_and(y == 1, n == 1))
        def _():
            post_all(32, B)

        @pl.when(jnp.logical_and(y == 3, later))
        def _():
            loc[n, 0] = apply([(block(PIV, 0), xin.at[n, 0])])
            down_rest(n, loc)
            tmp[0] = apply([(block(UP, 0), loc.at[n, 1])])
            mine[n] = loc[n, 0] - apply([(block(PIV, 0), tmp.at[0])])
            send(mine.at[n], zin.at[n], up_send.at[n], up_recv.at[n], (y - 1, p)).start()

        @pl.when(jnp.logical_and(y == 3, n < 2))
        def _():
            form(jnp.where(later, 38, 0), jnp.where(later, B, 22), jnp.where(later, B, 18))

        @pl.when(jnp.logical_and(y == 3, later))
        def _():
            red_middle(n - 1)

        @pl.when(has_down)
        def _():
            send_carry(n).wait_recv()

            @pl.when(jnp.logical_and(y == 2, down_short))
            def _():
                send_far(n).wait_recv()
                gsum[...] = gin[n] + far[n]

            @pl.when(jnp.logical_not(jnp.logical_and(y == 2, down_short)))
            def _():
                gsum[...] = gin[n]

            tmp[1] = xin[n, 0] - apply([(block(LOW, 0), gsum)])
            g[n, 0] = apply([(block(PIV, 0), tmp.at[1])])
            down_rest(n, g)

        @pl.when(jnp.logical_or(y == 2, jnp.logical_and(y == 1, jnp.logical_not(down_short))))
        def _():
            send_carry(n).start()

        @pl.when(jnp.logical_and(y == 1, n == 0))
        def _():
            form(0, 36, 20)

        @pl.when(jnp.logical_and(later, y < 2))
        def _():
            red_middle(n - 1)

        @pl.when(has_up)
        def _():
            send_up(n).wait_recv()

            @pl.when(jnp.logical_and(y == 2, later))
            def _():
                @pl.when(n == 1)
                def _():
                    pltpu.make_async_copy(held, held, over_recv).wait()

                gsum[...] = apply([((held, B), g.at[n, 1])], zin[n])

            @pl.when(jnp.logical_not(jnp.logical_and(y == 2, later)))
            def _():
                gsum[...] = zin[n]

            bacc[1] = apply([(block(UP, 1), gsum)])
            z[n, 1] = g[n, 1] - apply([(block(PIV, 1), bacc.at[1])])
            send_low(n).start()

        @pl.when(jnp.logical_not(has_up))
        def _():
            bacc[1] = jnp.zeros((B, 128), F32)
            z[n, 1] = g[n, 1]

        @pl.when(has_west)
        def _():
            send_west(n, 1).start()

        @pl.when(has_east)
        def _():
            send_east(n, 1).start()

        bacc[0] = apply([(block(UP, 0), z.at[n, 1])])
        z[n, 0] = g[n, 0] - apply([(block(PIV, 0), bacc.at[0])])

        @pl.when(jnp.logical_or(jnp.logical_or(y == 1, y == 2), jnp.logical_and(y == 3, n == 0)))
        def _():
            send_up(n).start()

        @pl.when(has_west)
        def _():
            send_west(n, 0).start()

        @pl.when(has_east)
        def _():
            send_east(n, 0).start()

        @pl.when(jnp.logical_and(y == 2, later))
        def _():
            red_middle(n - 1)

        @pl.when(jnp.logical_and(forms, n == 0))
        def _():
            post_all(jnp.where(y == 1, 20, 18), jnp.where(y == 1, 32, 22))
            form(jnp.where(y == 1, 36, 22), jnp.where(y == 1, B, 38), jnp.where(y == 1, 0, B))


        bacc[1] = apply([(block(DIAG, 1), z.at[n, 1]), (block(LOW, 1), z.at[n, 0])], bacc[1])
        bacc[0] = apply([(block(DIAG, 0), z.at[n, 0])], bacc[0])

        @pl.when(later)
        def _():
            red_end(n - 1)

        for k in range(2):
            u[n, k] = combined(xin[n, k], lambda i: u[i, k])
            d[n, k] = combined(z[n, k], lambda i: d[i, k])

        def halo(k):
            @pl.when(has_west)
            def _():
                send_east(n, k).wait_recv()

            @pl.when(has_east)
            def _():
                send_west(n, k).wait_recv()

        halo(1)
        value = apply([(block(WEST, 1), hw.at[n, 1]), (block(EAST, 1), he.at[n, 1])], bacc[1])
        xin[n + 1, 1] = combined(value, lambda i: xin[i + 1, 1])

        @pl.when(has_down)
        def _():
            send_low(n).wait_recv()
            bacc[0] = apply([(block(LOW, 0), zlow.at[n])], bacc[0])

        halo(0)
        value = apply([(block(WEST, 0), hw.at[n, 0]), (block(EAST, 0), he.at[n, 0])], bacc[0])
        xin[n + 1, 0] = combined(value, lambda i: xin[i + 1, 0])
        return carry

    lax.fori_loop(0, N, stage, 0)
    red_start(N - 1)

    zero = jnp.zeros((8, 128), F32)

    def entry(m, i):
        return res[m, pl.ds(i, 8, stride=0), :]

    size = [jnp.sqrt(gam[i]) for i in range(N - 1)]
    turns = []
    upper = {}
    target = [size[0]] + [zero] * N

    def column(m, below):
        value = [entry(m, i) / (size[i] * size[m]) for i in range(m + 1)] + [below]
        for k, (cosine, sine) in enumerate(turns):
            value[k], value[k + 1] = (
                cosine * value[k] + sine * value[k + 1],
                cosine * value[k + 1] - sine * value[k],
            )
        radius = jnp.sqrt(value[m] * value[m] + below * below)
        turns.append((value[m] / radius, below / radius))
        cosine, sine = turns[m]
        value[m] = cosine * value[m] + sine * below
        target[m], target[m + 1] = (
            cosine * target[m] + sine * target[m + 1],
            cosine * target[m + 1] - sine * target[m],
        )
        for i in range(m + 1):
            upper[i, m] = value[i]

    for m in range(N - 2):
        column(m, size[m + 1] * jnp.sqrt(entry(m, 5)) / size[m])
    red_middle(N - 1)
    red_end(N - 1)
    size.append(jnp.sqrt(gam[N - 1]))
    column(N - 2, size[N - 1] * jnp.sqrt(entry(N - 2, 5)) / size[N - 2])
    rest = entry(N - 1, 5)
    for i in range(N):
        rest = rest - entry(N - 1, i) * entry(N - 1, i) / gam[i]
    column(N - 1, jnp.sqrt(jnp.maximum(rest, 0.0)) / size[N - 1])
    answer = [None] * N
    for i in reversed(range(N)):
        value = target[i]
        for k in range(i + 1, N):
            value = value - upper[i, k] * answer[k]
        answer[i] = value / upper[i, i]
    for k in range(2):
        total = jnp.zeros((6, 8, 128), F32)
        for i in range(N):
            total = total + (answer[i] / size[i])[None] * d[i, k].reshape(6, 8, 128)
        out_ref[k] = total.reshape(B, 128)

    def drain(n, carry):
        @pl.when(has_up)
        def _():
            send_carry(n).wait_send()
            send_low(n).wait_send()

        @pl.when(has_down)
        def _():
            send_up(n).wait_send()

        for k in range(2):
            @pl.when(has_west)
            def _():
                send_west(n, k).wait_send()

            @pl.when(has_east)
            def _():
                send_east(n, k).wait_send()

        @pl.when(jnp.logical_and(y == 0, n > 1))
        def _():
            send_far(n).wait_send()

        pltpu.make_async_copy(recv1.at[n], recv1.at[n], red1_send.at[n]).wait()
        pltpu.make_async_copy(recv2.at[n], recv2.at[n], red2_send.at[n]).wait()
        return carry

    lax.fori_loop(0, N, drain, 0)

    @pl.when(forms)
    def _():
        pltpu.make_async_copy(over, over, over_send).wait()


def solution(mesh):
    lines, rows = mesh.shape["line"], mesh.shape["patch"]
    dma = pltpu.SemaphoreType.DMA
    pair = pltpu.VMEM((N, 2, B, 128), F32)
    single = pltpu.VMEM((N, B, 128), F32)
    tile = pltpu.VMEM((N, 8, 128), F32)
    tiles = pltpu.VMEM((N, GROUP - 1, 8, 128), F32)

    def per_device(newton_residual, diag_block, lower, upper, west, east, pivot_inverse):
        arrays = [a.reshape(2, B, B, 128) for a in (pivot_inverse, lower, upper, diag_block, west, east)]
        step = pl.pallas_call(
            functools.partial(kernel, lines, rows),
            out_shape=jax.ShapeDtypeStruct((2, B, 128), F32),
            in_specs=[pl.BlockSpec(memory_space=pl.ANY)] * 7,
            out_specs=pl.BlockSpec(memory_space=pltpu.VMEM),
            scratch_shapes=[
                pltpu.VMEM((6, 2, B, B, 128), jnp.bfloat16),
                pltpu.VMEM((6, 2, B * PITCH, 128), F32),
                pltpu.VMEM((N + 1, 2, B, 128), F32),
                pair, pair, pair, pair,
                single, single, single,
                pair, pair,
                pltpu.VMEM((2, B, 128), F32), pltpu.VMEM((2, B, 128), F32),
                tile, tiles, tile, tiles, tile,
                tile, tile,
                pltpu.VMEM((8, 128), F32),
                pltpu.VMEM((B * B, 128), F32), pltpu.VMEM((B * B, 128), F32),
                single, single, pair,
                pltpu.VMEM((3, B, 128), F32), pltpu.VMEM((B, 128), F32),
                dma((7, 2)),
                dma((N,)), dma((N,)), dma((N,)), dma((N,)), dma((N,)), dma((N,)),
                dma((N, 2)), dma((N, 2)), dma((N, 2)), dma((N, 2)),
                dma((N,)), dma((N,)), dma((N,)), dma((N,)),
                dma, dma, dma((N,)), dma((N,)),
            ],
            compiler_params=pltpu.CompilerParams(collective_id=0, has_side_effects=True),
        )(newton_residual.reshape(2, B, 128), *arrays)
        return (step * (1.0 / SCALE)).reshape(2, B, 1, 128)

    mats = P("line", None, None, "patch", None)
    return jax.shard_map(
        per_device,
        mesh=mesh,
        in_specs=(P("line", None, "patch", None), mats, mats, mats, mats, mats, mats),
        out_specs=P("line", None, "patch", None),
        check_vma=False,
    )
```
